128 devices in a mesh: rep: 2 (over core), dom: 64 (over y, z, x).
Axes of the slice: x: 4, y: 4, z: 4, core: 2. Of those that a mesh axis runs over, the one named last changes fastest.
Arguments:
- features: bfloat16 [8192, 512], P('dom'), may hold values from -6 to 6
- tiles: bfloat16 [8192, 128, 128], P(('rep', 'dom')), may hold values from -0.359375 to 0.359375
- tile_dest: int32 [8192, 1], P(('rep', 'dom')), may hold values from 0 to 63; in each aligned block of 64 rows (0 to 63, 64 to 127, ...) at most 2 rows name the same one
- tile_count: int32 [8192], P(('rep', 'dom')), may hold values from 16 to 128
- weight: bfloat16 [512, 512], replicated, may hold values from -0.25 to 0.25
- bias: float32 [512], replicated, may hold values from -3 to 3
- cotangent: bfloat16 [8192, 512], P('dom'), may hold values from -6 to 6
Outputs:
- activated: bfloat16 [8192, 512], P('dom', 'rep')
- weight_grad: float32 [512, 512], P(None, 'rep')
- feature_grad: bfloat16 [8192, 512], P('dom', 'rep')
The draws below stay inside these ranges and needn't reach their ends.
Inputs may be any that keep to these rules, and one draw needn't show every extreme that they name: `tile_dest`: among the tiles of one device no block is named more than 2 times, and some block is named exactly 2 times.
All inputs are finite; a program needn't handle non-finite values.
Results may differ from the reference program's by a relative error of at most 0.02.
Values may be sent and summed in bfloat16 or wider, within the bound.
A program may use at most 128 MiB of HBM per device.

```python
import math
import jax
import jax.numpy as jnp
import numpy as np
from jax import lax

F = 512
BLK = 128
TILES_DEV = 64
CAP = 2
NODES = 8192
TILES = 8192
N_DOM = 64


def with_ends(drawn, rng, least, high):
    spot = [jax.random.randint(jax.random.fold_in(rng, axis), (), 0, length) for axis, length in enumerate(drawn.shape)]
    main_axis = drawn.shape.index(max(drawn.shape))
    next_to = spot[:main_axis] + [(spot[main_axis] + 1) % drawn.shape[main_axis]] + spot[main_axis + 1:]
    return drawn.at[tuple(spot)].set(least).at[tuple(next_to)].set(high)


def shard_levels(own_key, shape, pieces, low, top_value):
    def one(position, shards_of):
        steps = jax.random.uniform(jax.random.fold_in(jax.random.fold_in(own_key, 6), position), (shards_of,), jnp.float32, low / len(pieces), top_value / len(pieces))
        return jnp.repeat(jnp.exp(steps), shape[position] // shards_of).reshape((-1,) + (1,) * (len(shape) - position - 1))

    loudness = one(*pieces[0])
    for cut in pieces[1:]:
        loudness = loudness * one(*cut)
    return loudness


def deal_out(stream_key, own, number, rows, number_of, top, bound, lean):
    ranking = jax.random.permutation(stream_key, number_of)
    packed, usual = load_shares(number_of, rows * top, bound, lean, True), load_shares(number_of, rows * top, bound, lean, False)
    places = jnp.arange(number_of)

    def named(lengths, rotation):
        used = int((lengths > 0).sum())
        fixed = max(1, used // 4)
        moved = fixed + (places - fixed + rotation * (used - fixed)) % max(1, number_of - fixed)
        return jnp.zeros((number_of,), jnp.int32).at[ranking[jnp.where(places < fixed, places, moved)]].set(jnp.asarray(lengths, jnp.int32))

    lengths = jnp.where(number % 4 == 0, named(packed, number // 4), named(usual, number - number // 4 - 1))
    mixed = jax.random.permutation(jax.random.fold_in(own, 3), number_of)
    giver, receiver = mixed[0:number_of // 2 * 2:2], mixed[1:number_of // 2 * 2:2]
    slack = jnp.minimum(lengths[giver] - 1, bound - lengths[receiver]) // 2
    slack = jnp.where((giver == ranking[0]) | (receiver == ranking[0]) | (lengths[receiver] == 0), 0, jnp.maximum(slack, 0))
    moved = jax.random.randint(jax.random.fold_in(own, 4), (number_of // 2,), 0, 1 << 20) % (slack + 1)
    lengths = lengths.at[giver].add(-moved).at[receiver].add(moved)
    items = jnp.searchsorted(jnp.cumsum(lengths), jnp.arange(rows * top), side="right").astype(jnp.int32)
    grid = items.reshape(top, rows).T
    grid = grid[jax.random.permutation(jax.random.fold_in(own, 1), rows)]
    rotation = jax.random.randint(jax.random.fold_in(own, 2), (rows, 1), 0, top)
    return jnp.take_along_axis(grid, (jnp.arange(top)[None, :] + rotation) % top, axis=1)


def load_shares(number_of, total, limit, slope, full):
    portions = [(1 << 20) // math.isqrt(rank ** slope) + 1 for rank in range(1, number_of + 1)]
    largest = limit if full else min(limit, max(-(-total // number_of), total * portions[0] // sum(portions)))
    least = 1 if total - largest >= number_of - 1 else 0
    given, surplus = [largest] + [least] * (number_of - 1), total - largest - least * (number_of - 1)
    while surplus > 0:
        candidates = [i for i in range(1, number_of) if given[i] < largest] or [i for i in range(1, number_of) if given[i] < limit]
        pool, remaining = sum([portions[i] for i in candidates]), surplus
        for i in candidates:
            more = min(limit - given[i], max(1, remaining * portions[i] // pool), surplus)
            given[i] = given[i] + more
            surplus = surplus - more
    return np.array(given)


def gaussian(stream_key, shape, deviation, most, cuts=(), held_as=jnp.bfloat16):
    drawn = jax.random.normal(stream_key, shape, jnp.float32) * deviation
    if len(cuts) > 0:
        drawn = shard_levels(stream_key, shape, cuts, -0.22, 0.18) * drawn
    return jnp.clip(drawn, min=-most, max=most).astype(held_as)


def setup_inputs(seed: int = 0) -> dict:
    key_list = jax.random.split(jax.random.key(seed), 8)
    features = gaussian(key_list[0], (NODES, F), 1.0, 6.0, ((0, 64),))
    tiles = gaussian(key_list[1], (TILES, BLK, BLK), 0.06, 0.359375, ((0, 128),))
    tile_dest_keys = jax.random.split(jax.random.fold_in(key_list[2], 1), TILES // TILES_DEV)
    tile_dest_turns = jax.random.permutation(jax.random.fold_in(key_list[2], 3), TILES // TILES_DEV)
    tile_dest = jax.vmap(lambda own, number: deal_out(jax.random.fold_in(key_list[2], 2), own, number, TILES_DEV, N_DOM, 1, CAP, 1))(tile_dest_keys, tile_dest_turns).reshape((TILES, 1))
    tile_count = with_ends(jax.random.randint(key_list[3], (TILES,), 16, 129), jax.random.fold_in(key_list[3], 1), 16, 128).astype(jnp.int32)
    weight = gaussian(key_list[4], (F, F), F ** -0.5, 0.25)
    bias = gaussian(key_list[5], (F,), 0.5, 3.0, (), jnp.float32)
    cotangent = gaussian(key_list[6], (NODES, F), 1.0, 6.0, ((0, 64),))
    return {"features": features, "tiles": tiles, "tile_dest": tile_dest, "tile_count": tile_count, "weight": weight, "bias": bias, "cotangent": cotangent}


def reference(features, tiles, tile_dest, tile_count, weight, bias, cotangent):
    shards = 2 * N_DOM
    blocks = features.reshape(N_DOM, BLK, F).astype(jnp.float32)
    tile_sets = tiles.reshape(shards, TILES_DEV, BLK, BLK)
    dest_sets = tile_dest.reshape(shards, TILES_DEV).astype(jnp.int32)
    scale_sets = lax.rsqrt(tile_count.astype(jnp.float32)).reshape(shards, TILES_DEV)
    source_ids = (jnp.arange(shards, dtype=jnp.int32) % N_DOM).astype(jnp.int32)

    def forward_step(total, item):
        tile_set, dest_set, scale_set, source = item
        panel = blocks[source]
        terms = jnp.einsum('tij,jf->tif', tile_set.astype(jnp.float32), panel) * scale_set[:, None, None]
        rounded = lax.optimization_barrier(terms.astype(jnp.bfloat16))
        return (total.at[dest_set].add(rounded.astype(jnp.float32)), None)
    start = jnp.zeros((N_DOM, BLK, F), jnp.float32)
    summed, _ = lax.scan(forward_step, start, (tile_sets, dest_sets, scale_sets, source_ids))
    aggregated = summed.reshape(NODES, F).astype(jnp.bfloat16)
    pre = jnp.dot(aggregated, weight, preferred_element_type=jnp.float32) + bias
    sig = jax.nn.sigmoid(pre)
    activated = (pre * sig).astype(jnp.bfloat16)
    pre_grad = (cotangent.astype(jnp.float32) * sig * (1.0 + pre * (1.0 - sig))).astype(jnp.bfloat16)
    weight_grad = jnp.dot(aggregated.T, pre_grad, preferred_element_type=jnp.float32) / jnp.sqrt(jnp.float32(NODES))
    row_grad = jnp.dot(pre_grad, weight.T, preferred_element_type=jnp.float32).astype(jnp.bfloat16)
    grad_blocks = row_grad.reshape(N_DOM, BLK, F).astype(jnp.float32)

    def backward_step(total, item):
        tile_set, dest_set, scale_set, source = item
        picked = grad_blocks[dest_set]
        terms = jnp.einsum('tij,tif->tjf', tile_set.astype(jnp.float32), picked) * scale_set[:, None, None]
        return (total.at[source].add(lax.optimization_barrier(jnp.sum(terms, axis=0))), None)
    back, _ = lax.scan(backward_step, jnp.zeros((N_DOM, BLK, F), jnp.float32), (tile_sets, dest_sets, scale_sets, source_ids))
    feature_grad = back.reshape(NODES, F).astype(jnp.bfloat16)
    return (activated, weight_grad, feature_grad)
```

```python
import jax
import jax.numpy as jnp
from jax import lax
from jax.experimental import pallas as pl
from jax.experimental.pallas import tpu as pltpu
from jax.sharding import PartitionSpec as P


def build_blocks(dest_ref, count_ref, tiles_ref, out_ref, which, used):
    blocks = out_ref.shape[0]

    @pl.loop(0, blocks)
    def _(b):
        used[b] = 0
        which[2 * b] = 0
        which[2 * b + 1] = 0

    @pl.loop(0, tiles_ref.shape[0])
    def _(t):
        d = dest_ref[t]
        k = used[d]
        which[2 * d + k] = t
        used[d] = k + 1

    @pl.loop(0, blocks)
    def _(b):
        n = used[b]
        total = jnp.zeros(out_ref.shape[1:], jnp.float32)
        for k in range(2):
            t = which[2 * b + k]
            c = jnp.full((8, 128), jnp.maximum(count_ref[t], 1), jnp.int32).astype(jnp.float32)
            s = jnp.where(n > k, lax.rsqrt(c), 0.0)[0:1, :]
            total = total + tiles_ref[t].astype(jnp.float32) * s
        out_ref[b] = total.astype(out_ref.dtype)


def adjacency(tiles, dest, count, domains):
    shape = (domains,) + tiles.shape[1:]
    return pl.pallas_call(
        build_blocks,
        out_shape=jax.ShapeDtypeStruct(shape, jnp.bfloat16),
        in_specs=[
            pl.BlockSpec(memory_space=pltpu.SMEM),
            pl.BlockSpec(memory_space=pltpu.SMEM),
            pl.BlockSpec(memory_space=pltpu.VMEM),
        ],
        out_specs=pl.BlockSpec(memory_space=pltpu.VMEM),
        scratch_shapes=[pltpu.SMEM((2 * domains,), jnp.int32), pltpu.SMEM((domains,), jnp.int32)],
        name="adjacency",
    )(dest, count, tiles)


def per_device(features, tiles, tile_dest, tile_count, weight, bias, cotangent):
    domains = lax.axis_size("dom")
    r = lax.axis_index("rep")
    block, width = features.shape
    half = width // 2
    own = adjacency(tiles, tile_dest[:, 0], tile_count, domains)
    both = lax.all_gather(own, "rep", axis=0)
    feat = lax.dynamic_slice_in_dim(features, r * half, half, 1)
    partial = jnp.einsum("rbij,jf->bif", both, feat, preferred_element_type=jnp.float32)
    received = lax.all_to_all(
        partial.astype(jnp.bfloat16), "dom", split_axis=0, concat_axis=0, tiled=True
    )
    agg_half = jnp.sum(received, axis=0, dtype=jnp.float32).astype(jnp.bfloat16)
    agg = lax.all_gather(agg_half, "rep", axis=1, tiled=True)
    pre = jnp.dot(agg, weight, preferred_element_type=jnp.float32) + bias
    sig = jax.nn.sigmoid(pre)
    activated = lax.dynamic_slice_in_dim(pre * sig, r * half, half, 1).astype(jnp.bfloat16)
    pre_grad = (cotangent.astype(jnp.float32) * sig * (1.0 + pre * (1.0 - sig))).astype(
        jnp.bfloat16
    )
    grad_half = lax.dynamic_slice_in_dim(pre_grad, r * half, half, 1)
    w_half = lax.dynamic_slice_in_dim(weight, r * half, half, 0)
    row_grad = lax.dot_general(
        pre_grad, w_half, (((1,), (1,)), ((), ())), preferred_element_type=jnp.float32
    ).astype(jnp.bfloat16)
    every = lax.all_gather(row_grad, "dom", axis=0, tiled=True).reshape(domains, block, half)
    weight_part = jnp.dot(agg.T, grad_half, preferred_element_type=jnp.float32)
    weight_grad = lax.psum(weight_part, "dom") / jnp.sqrt(jnp.float32(domains * block))
    back = jnp.einsum("rbij,bif->jf", both, every, preferred_element_type=jnp.float32)
    return (activated, weight_grad, back.astype(jnp.bfloat16))


def solution(mesh):
    in_specs = (
        P("dom", None),
        P(("rep", "dom"), None, None),
        P(("rep", "dom"), None),
        P(("rep", "dom")),
        P(),
        P(),
        P("dom", None),
    )
    out_specs = (P("dom", "rep"), P(None, "rep"), P("dom", "rep"))
    return jax.shard_map(
        per_device, mesh=mesh, in_specs=in_specs, out_specs=out_specs, check_vma=False
    )
```

```python
import math

import jax
import jax.numpy as jnp
from jax import lax
from jax.experimental import pallas as pl
from jax.experimental.pallas import tpu as pltpu
from jax.sharding import PartitionSpec as P


def build_blocks(dest_ref, count_ref, tiles_ref, out_ref, which, used):
    blocks = out_ref.shape[0]

    @pl.loop(0, blocks)
    def _(b):
        used[b] = 0
        which[2 * b] = 0
        which[2 * b + 1] = 0

    @pl.loop(0, tiles_ref.shape[0])
    def _(t):
        d = dest_ref[t]
        k = used[d]
        which[2 * d + k] = t
        used[d] = k + 1

    @pl.loop(0, blocks)
    def _(b):
        n = used[b]
        total = jnp.zeros(out_ref.shape[1:], jnp.float32)
        for k in range(2):
            t = which[2 * b + k]
            c = jnp.full((8, 128), jnp.maximum(count_ref[t], 1), jnp.int32).astype(jnp.float32)
            s = jnp.where(n > k, lax.rsqrt(c), 0.0)[0:1, :]
            total = total + tiles_ref[t].astype(jnp.float32) * s
        out_ref[b] = total.astype(out_ref.dtype)


def adjacency(tiles, dest, count, domains):
    shape = (domains,) + tiles.shape[1:]
    return pl.pallas_call(
        build_blocks,
        out_shape=jax.ShapeDtypeStruct(shape, jnp.bfloat16),
        in_specs=[
            pl.BlockSpec(memory_space=pltpu.SMEM),
            pl.BlockSpec(memory_space=pltpu.SMEM),
            pl.BlockSpec(memory_space=pltpu.VMEM),
        ],
        out_specs=pl.BlockSpec(memory_space=pltpu.VMEM),
        scratch_shapes=[pltpu.SMEM((2 * domains,), jnp.int32), pltpu.SMEM((domains,), jnp.int32)],
        name="adjacency",
    )(dest, count, tiles)


ROWS = ((0, 48), (48, 48), (96, 32))
STRIDE = (16, 4, 1)
MESH = pl.DeviceIdType.MESH


def layer_kernel(
    own_ref, feat_ref, weight_ref, bias_ref, cot_ref,
    act_ref, wgrad_ref, fgrad_ref,
    a2, at0, at1, at2, ff, p0, p1, p2, g0, g1, g2,
    ra0, ra1, ra2, rb0, rb1, rb2, rc0, rc1, rc2,
    agg, pg, actv, wp, wra, wrb, wrc, wg, acc,
    own_sem, swap_send, swap_recv, agg_send, agg_recv,
    rs_send, rs_recv, ag_send, ag_recv, ws_send, ws_recv, wa_send, wa_recv,
):
    r = lax.axis_index("rep")
    d = lax.axis_index("dom")
    other = 1 - r
    me = (d // 16, (d // 4) % 4, d % 4)
    P_ = (p0, p1, p2)
    G_ = (g0, g1, g2)
    AT = (at0, at1, at2)
    RV = ((ra0, ra1, ra2), (rb0, rb1, rb2), (rc0, rc1, rc2))
    f32, bf16 = jnp.float32, jnp.bfloat16
    started = []

    def near(a, o):
        c = (me[a] + o) % 4
        return c, (r, d + (c - me[a]) * STRIDE[a])

    barrier = pltpu.get_barrier_semaphore()
    pl.semaphore_signal(barrier, inc=1, device_id=(other, d), device_id_type=MESH)
    for a in range(3):
        for o in (1, 2, 3):
            pl.semaphore_signal(barrier, inc=1, device_id=near(a, o)[1], device_id_type=MESH)
    pl.semaphore_wait(barrier, 10)

    def remote(src, dst, ssem, rsem, dev):
        c = pltpu.make_async_remote_copy(
            src_ref=src, dst_ref=dst, send_sem=ssem, recv_sem=rsem,
            device_id=dev, device_id_type=MESH,
        )
        c.start()
        started.append(c)
        return c

    half = 256
    cols = pl.ds(pl.multiple_of(r * half, half), half)
    swaps, locals_ = [], []
    for i in range(4):
        swaps.append(
            remote(own_ref.at[i], a2.at[i, :, :, :, 128:256], swap_send.at[i], swap_recv.at[i], (other, d))
        )
        c = pltpu.make_async_copy(own_ref.at[i], a2.at[i, :, :, :, 0:128], own_sem.at[i])
        c.start()
        locals_.append(c)
    ff[0:128, :] = feat_ref[:, cols]
    ff[128:256, :] = feat_ref[:, cols]

    for i in range(4):
        locals_[i].wait()
        swaps[i].wait_recv()

        def forward(j, _):
            lhs = a2[i, j].reshape(512, 256)
            res = jnp.dot(lhs, ff[...], preferred_element_type=f32).astype(bf16)
            res = res.reshape(4, 128, 256)
            for k, (lo, n) in enumerate(ROWS):
                for h in range(2):
                    P_[k][i, j, :, h] = res[:, lo : lo + n, 128 * h : 128 * h + 128]
            return 0

        lax.fori_loop(0, 4, forward, 0)

    def view(fixed, h):
        return tuple(fixed.get(a, slice(None)) for a in range(3)) + (h,)

    def rs_open(k, j):
        axes = [(k + i) % 3 for i in range(3)]
        a = axes[j]
        fixed = {axes[i]: me[axes[i]] for i in range(j)}
        rv = RV[j][k]
        src = P_[k]
        out = []
        for w, (sign, h1) in enumerate(((1, 0), (3, 1))):
            c1, dev = near(a, sign)
            c2, _ = near(a, 2)
            first = remote(
                src.at[view({**fixed, a: c2}, h1)], rv.at[w, 0],
                rs_send.at[k, j, w, 0], rs_recv.at[k, j, w, 0], dev,
            )
            second = remote(
                src.at[view({**fixed, a: c1}, 1 - h1)], rv.at[w, 1],
                rs_send.at[k, j, w, 1], rs_recv.at[k, j, w, 1], dev,
            )
            out.append((first, second, view({**fixed, a: c1}, h1), dev))
        return out

    def rs_pass(k, j, opened):
        rv = RV[j][k]
        src = P_[k]
        for w in range(2):
            first, second, where, dev = opened[w]
            first.wait_recv()
            src[where] = (src[where].astype(f32) + rv[w, 0].astype(f32)).astype(bf16)
            third = remote(
                src.at[where], rv.at[w, 2], rs_send.at[k, j, w, 2], rs_recv.at[k, j, w, 2], dev
            )
            opened[w] = (second, third)

    def rs_close(k, j, opened):
        rv = RV[j][k]
        src = P_[k]
        axes = [(k + i) % 3 for i in range(3)]
        fixed = {axes[i]: me[axes[i]] for i in range(j + 1)}
        for w in range(2):
            for c in opened[w]:
                c.wait_recv()
        for h in range(2):
            where = view(fixed, h)
            total = src[where].astype(f32) + rv[h, 2].astype(f32) + rv[1 - h, 1].astype(f32)
            if j < 2:
                src[where] = total.astype(bf16)
            else:
                lo, n = ROWS[k]
                agg[lo : lo + n, pl.ds(pl.multiple_of(r * half + 128 * h, 128), 128)] = total.astype(bf16)

    opened = [rs_open(k, 0) for k in range(3)]
    for k in range(3):
        for c in range(4):
            sel = tuple(c if a == k else slice(None) for a in range(3)) + (slice(*(ROWS[k][0], sum(ROWS[k]))),)
            AT[k][c] = a2[sel].reshape(16 * ROWS[k][1], 256).T
    for j in range(3):
        if j > 0:
            opened = [rs_open(k, j) for k in range(3)]
        for k in range(3):
            rs_pass(k, j, opened[k])
        for k in range(3):
            rs_close(k, j, opened[k])

    mine = agg.at[:, cols]
    swap = remote(mine, mine, agg_send.at[0], agg_recv.at[0], (other, d))
    swap.wait_recv()
    pre = jnp.dot(agg[...], weight_ref[...], preferred_element_type=f32) + bias_ref[...]
    sig = jax.nn.sigmoid(pre)
    pg[...] = (cot_ref[...].astype(f32) * sig * (1.0 + pre * (1.0 - sig))).astype(bf16)
    actv[...] = (pre * sig).astype(bf16)
    row_grad = lax.dot_general(
        pg[...], weight_ref[cols, :], (((1,), (1,)), ((), ())), preferred_element_type=f32
    ).astype(bf16)
    for k, (lo, n) in enumerate(ROWS):
        for h in range(2):
            G_[k][me[0], me[1], me[2], h] = row_grad[lo : lo + n, 128 * h : 128 * h + 128]

    def ag_axes(k, j):
        axes = [(k + 2 - i) % 3 for i in range(3)]
        return axes[j], {axes[i]: me[axes[i]] for i in range(j + 1, 3)}

    def ag_open(k, j):
        a, fixed = ag_axes(k, j)
        out = []
        for w, (sign, h1) in enumerate(((1, 0), (3, 1))):
            _, dev = near(a, sign)
            c = []
            for m, h in enumerate((h1, 1 - h1)):
                ref = G_[k].at[view({**fixed, a: me[a]}, h)]
                c.append(remote(ref, ref, ag_send.at[k, j, w, m], ag_recv.at[k, j, w, m], dev))
            out.append(c)
        return out

    def ag_pass(k, j, opened):
        a, fixed = ag_axes(k, j)
        for w, (sign, h1) in enumerate(((1, 0), (3, 1))):
            _, dev = near(a, sign)
            origin, _ = near(a, 4 - sign)
            opened[w][0].wait_recv()
            ref = G_[k].at[view({**fixed, a: origin}, h1)]
            opened[w].append(remote(ref, ref, ag_send.at[k, j, w, 2], ag_recv.at[k, j, w, 2], dev))

    def ag_close(k, j, opened):
        for w in range(2):
            opened[w][1].wait_recv()
        for w in range(2):
            opened[w][2].wait_recv()

    WR = (wra, wrb, wrc)
    WS_AXES = (0, 1, 2)
    WA_AXES = (0, 2, 1)

    def wview(fixed):
        return tuple(fixed.get(a, slice(None)) for a in range(3))

    def ws_open(j):
        a = WS_AXES[j]
        fixed = {WS_AXES[i]: me[WS_AXES[i]] for i in range(j)}
        out = []
        for o in (1, 3, 2):
            c, dev = near(a, o)
            out.append(
                remote(wp.at[wview({**fixed, a: c})], WR[j].at[o - 1], ws_send.at[j, o - 1], ws_recv.at[j, o - 1], dev)
            )
        return out

    def ws_close(j, opened):
        for c in opened:
            c.wait_recv()
        where = wview({WS_AXES[i]: me[WS_AXES[i]] for i in range(j + 1)})
        total = wp[where].astype(f32)
        for o in range(3):
            total = total + WR[j][o].astype(f32)
        (wp if j < 2 else wg)[where] = total.astype(bf16)

    def wa_open(j):
        a = WA_AXES[j]
        fixed = {WA_AXES[i]: me[WA_AXES[i]] for i in range(j, 3)}
        ref = wg.at[wview(fixed)]
        out = []
        for o in (1, 3, 2):
            _, dev = near(a, o)
            out.append(remote(ref, ref, wa_send.at[j, o - 1], wa_recv.at[j, o - 1], dev))
        return out

    def wa_close(opened):
        for c in opened:
            c.wait_recv()

    gather = [ag_open(k, 0) for k in range(3)]
    part = lax.dot_general(
        agg[...], pg[:, cols], (((0,), (0,)), ((), ())), preferred_element_type=f32
    ).astype(bf16)
    for h in range(2):
        wp[2 * h : 2 * h + 2] = part[:, 128 * h : 128 * h + 128].reshape(2, 4, 4, 16, 128)
    w = ws_open(0)
    act_ref[...] = actv[:, cols]
    for k in range(3):
        ag_pass(k, 0, gather[k])
    for k in range(3):
        ag_close(k, 0, gather[k])
    gather = [ag_open(k, 1) for k in range(3)]
    ws_close(0, w)
    w = ws_open(1)
    for k in range(3):
        ag_pass(k, 1, gather[k])
    ws_close(1, w)
    w = ws_open(2)
    for k in range(3):
        ag_close(k, 1, gather[k])
    gather = [ag_open(k, 2) for k in range(3)]
    ws_close(2, w)
    w = wa_open(0)

    acc[...] = jnp.zeros_like(acc)

    def backward(k, o):
        c, _ = near(k, o)
        n = 16 * ROWS[k][1]
        lhs = AT[k][c]
        for h in range(2):
            rhs = G_[k][view({k: c}, h)].reshape(n, 128)
            acc[:, 128 * h : 128 * h + 128] += jnp.dot(lhs, rhs, preferred_element_type=f32)

    for k in range(3):
        ag_pass(k, 2, gather[k])
    wa_close(w)
    w = wa_open(1)
    for k in range(3):
        backward(k, 0)
    for k in range(3):
        for q in range(2):
            gather[k][q][1].wait_recv()
    wa_close(w)
    w = wa_open(2)
    for k in range(3):
        backward(k, 1)
        backward(k, 3)
    for k in range(3):
        for q in range(2):
            gather[k][q][2].wait_recv()
    for k in range(3):
        backward(k, 2)
    fgrad_ref[...] = (acc[0:128, :] + acc[128:256, :]).astype(bf16)
    wa_close(w)
    norm = 1.0 / math.sqrt(8192.0)
    for h in range(2):
        full = wg[2 * h : 2 * h + 2].reshape(512, 128).astype(f32) * norm
        wgrad_ref[:, 128 * h : 128 * h + 128] = full
    for c in started:
        c.wait_send()


def layer(own, feat, weight, bias, cot):
    bf16, f32 = jnp.bfloat16, jnp.float32
    V = pltpu.VMEM
    dma = pltpu.SemaphoreType.DMA
    sizes = [n for _, n in ROWS]
    scratch = [V((4, 4, 4, 128, 256), bf16)]
    scratch += [V((4, 256, 16 * n), bf16) for n in sizes]
    scratch += [V((256, 256), bf16)]
    scratch += [V((4, 4, 4, 2, n, 128), bf16) for n in sizes]
    scratch += [V((4, 4, 4, 2, n, 128), bf16) for n in sizes]
    scratch += [V((2, 3, 4, 4, n, 128), bf16) for n in sizes]
    scratch += [V((2, 3, 4, n, 128), bf16) for n in sizes]
    scratch += [V((2, 3, n, 128), bf16) for n in sizes]
    scratch += [V((128, 512), bf16)] * 3
    scratch += [V((4, 4, 4, 16, 128), bf16)]
    scratch += [V((3, 4, 4, 16, 128), bf16), V((3, 4, 16, 128), bf16), V((3, 16, 128), bf16)]
    scratch += [V((4, 4, 4, 16, 128), bf16), V((256, 256), f32)]
    scratch += [dma((4,)), dma((4,)), dma((4,)), dma((1,)), dma((1,))]
    scratch += [dma((3, 3, 2, 3))] * 4 + [dma((3, 3))] * 4
    whole = pl.BlockSpec(memory_space=pltpu.VMEM)
    return pl.pallas_call(
        layer_kernel,
        out_shape=[
            jax.ShapeDtypeStruct((128, 256), bf16),
            jax.ShapeDtypeStruct((512, 256), f32),
            jax.ShapeDtypeStruct((128, 256), bf16),
        ],
        in_specs=[pl.BlockSpec(memory_space=pl.ANY)] + [whole] * 4,
        out_specs=[whole] * 3,
        scratch_shapes=scratch,
        compiler_params=pltpu.CompilerParams(collective_id=0, has_side_effects=True),
        name="layer",
    )(own, feat, weight, bias, cot)


def per_device(features, tiles, tile_dest, tile_count, weight, bias, cotangent):
    domains = lax.axis_size("dom")
    own = adjacency(tiles, tile_dest[:, 0], tile_count, domains)
    own = own.reshape(4, 4, 4, 128, 128)
    act, wgrad, fgrad = layer(own, features, weight, bias.reshape(1, -1), cotangent)
    return act, wgrad, fgrad


def solution(mesh):
    in_specs = (
        P("dom", None),
        P(("rep", "dom"), None, None),
        P(("rep", "dom"), None),
        P(("rep", "dom")),
        P(),
        P(),
        P("dom", None),
    )
    out_specs = (P("dom", "rep"), P(None, "rep"), P("dom", "rep"))
    return jax.shard_map(
        per_device, mesh=mesh, in_specs=in_specs, out_specs=out_specs, check_vma=False
    )
```

```python
import math

import jax
import jax.numpy as jnp
from jax import lax
from jax.experimental import pallas as pl
from jax.experimental.pallas import tpu as pltpu
from jax.sharding import PartitionSpec as P


def build_blocks(dest_ref, count_ref, tiles_ref, out_ref, which, used):
    blocks = out_ref.shape[0]

    @pl.loop(0, blocks)
    def _(b):
        used[b] = 0
        which[2 * b] = 0
        which[2 * b + 1] = 0

    @pl.loop(0, tiles_ref.shape[0], unroll=8)
    def _(t):
        d = dest_ref[t]
        k = used[d]
        which[2 * d + k] = t
        used[d] = k + 1

    @pl.loop(0, blocks, unroll=4)
    def _(b):
        n = used[b]
        total = jnp.zeros(out_ref.shape[1:], jnp.float32)
        for k in range(2):
            t = which[2 * b + k]
            c = jnp.full((8, 128), jnp.maximum(count_ref[t], 1), jnp.int32).astype(jnp.float32)
            s = jnp.where(n > k, lax.rsqrt(c), 0.0)[0:1, :]
            total = total + tiles_ref[t].astype(jnp.float32) * s
        out_ref[b] = total.astype(out_ref.dtype)


def adjacency(tiles, dest, count, domains):
    shape = (domains,) + tiles.shape[1:]
    return pl.pallas_call(
        build_blocks,
        out_shape=jax.ShapeDtypeStruct(shape, jnp.bfloat16),
        in_specs=[
            pl.BlockSpec(memory_space=pltpu.SMEM),
            pl.BlockSpec(memory_space=pltpu.SMEM),
            pl.BlockSpec(memory_space=pltpu.VMEM),
        ],
        out_specs=pl.BlockSpec(memory_space=pltpu.VMEM),
        scratch_shapes=[pltpu.SMEM((2 * domains,), jnp.int32), pltpu.SMEM((domains,), jnp.int32)],
        name="adjacency",
    )(dest, count, tiles)


ROWS = ((0, 48), (48, 48), (96, 32))
STRIDE = (16, 4, 1)
MESH = pl.DeviceIdType.MESH


def layer_kernel(
    own_ref, feat_ref, weight_ref, bias_ref, cot_ref,
    act_ref, wsum_ref, fgrad_ref,
    a2, at0, at1, at2, ff, p0, p1, p2, g0, g1, g2,
    ra0, ra1, ra2, rb0, rb1, rb2, rc0, rc1, rc2,
    agg, pg, actv, wp, wra, wrb, wrc, wg, acc,
    own_sem, swap_send, swap_recv, agg_send, agg_recv,
    rs_send, rs_recv, rd_send, rd_recv, ad_send, ad_recv,
    ag_send, ag_recv, ws_send, ws_recv, wa_send, wa_recv,
):
    r = lax.axis_index("rep")
    d = lax.axis_index("dom")
    other = 1 - r
    me = (d // 16, (d // 4) % 4, d % 4)
    P_ = (p0, p1, p2)
    G_ = (g0, g1, g2)
    AT = (at0, at1, at2)
    RV = ((ra0, ra1, ra2), (rb0, rb1, rb2), (rc0, rc1, rc2))
    f32, bf16 = jnp.float32, jnp.bfloat16
    started = []

    def near(a, o):
        c = (me[a] + o) % 4
        return c, (r, d + (c - me[a]) * STRIDE[a])

    barrier = pltpu.get_barrier_semaphore()
    pl.semaphore_signal(barrier, inc=1, device_id=(other, d), device_id_type=MESH)
    for a in range(3):
        for o in (1, 2, 3):
            pl.semaphore_signal(barrier, inc=1, device_id=near(a, o)[1], device_id_type=MESH)
    pl.semaphore_wait(barrier, 10)

    def remote(src, dst, ssem, rsem, dev):
        c = pltpu.make_async_remote_copy(
            src_ref=src, dst_ref=dst, send_sem=ssem, recv_sem=rsem,
            device_id=dev, device_id_type=MESH,
        )
        c.start()
        started.append(c)
        return c

    half = 256
    cols = pl.ds(pl.multiple_of(r * half, half), half)
    ORDER = (2, 1, 3, 0)
    WAYS = ((1, 0), (3, 1))
    swaps, locals_ = [], []
    for s, o in enumerate(ORDER):
        i, _ = near(0, o)
        swaps.append(
            remote(own_ref.at[i], a2.at[i, :, :, :, 128:256], swap_send.at[s], swap_recv.at[s], (other, d))
        )
        c = pltpu.make_async_copy(own_ref.at[i], a2.at[i, :, :, :, 0:128], own_sem.at[s])
        c.start()
        locals_.append(c)
    ff[0:128, :] = feat_ref[:, cols]
    ff[128:256, :] = feat_ref[:, cols]

    def view(fixed, h):
        return tuple(fixed.get(a, slice(None)) for a in range(3)) + ((h,) if h is not None else ())

    def rs_axes(k):
        return [(k + i) % 3 for i in range(3)]

    def rs_fixed(k, j):
        axes = rs_axes(k)
        return axes[j], {axes[i]: me[axes[i]] for i in range(j)}

    def rs_send_of(k, j, w, m, extra):
        a, fixed = rs_fixed(k, j)
        sign, h1 = WAYS[w]
        c, _ = near(a, 2 if m == 0 else sign)
        _, dev = near(a, sign)
        h = h1 if m == 0 else 1 - h1
        spot = rv_view(k, j, w, m, extra)
        return dict(
            src_ref=P_[k].at[view({**fixed, a: c, **extra}, h)], dst_ref=RV[j][k].at[spot],
            send_sem=rs_send.at[k, j, w, m], recv_sem=rs_recv.at[k, j, w, m],
            device_id=dev, device_id_type=MESH,
        )

    def rv_view(k, j, w, m, extra):
        a, fixed = rs_fixed(k, j)
        left = [x for x in range(3) if x != a and x not in fixed]
        return (w, m) + tuple(extra.get(x, slice(None)) for x in left)

    def rs_open(k, j, w, m, extra=None):
        pltpu.make_async_remote_copy(**rs_send_of(k, j, w, m, extra or {})).start()

    def rs_whole(k, j, w, m):
        c = pltpu.make_async_remote_copy(**rs_send_of(k, j, w, m, {}))
        started.append(c)
        return c

    lag = None
    for s, o in enumerate(ORDER):
        i, _ = near(0, o)
        locals_[s].wait()
        swaps[s].wait_recv()

        def forward(j, _, i=i):
            lhs = a2[i, j].reshape(512, 256)
            res = jnp.dot(lhs, ff[...], preferred_element_type=f32).astype(bf16)
            res = res.reshape(4, 128, 256)
            for k, (lo, n) in enumerate(ROWS):
                for h in range(2):
                    P_[k][i, j, :, h] = res[:, lo : lo + n, 128 * h : 128 * h + 128]
            return 0

        lax.fori_loop(0, 4, forward, 0)
        if o == 2:
            rs_open(0, 0, 0, 0)
            rs_open(0, 0, 1, 0)
        elif o == 1:
            rs_open(0, 0, 0, 1)
        elif o == 3:
            rs_open(0, 0, 1, 1)
        for k in (1, 2):
            for w in range(2):
                rs_open(k, 0, w, 0, {0: i})
        for k in (1, 2):
            for w in range(2):
                if lag is not None:
                    rs_open(k, 0, w, 1, {0: lag})
        lag = i
    for k in (1, 2):
        for w in range(2):
            rs_open(k, 0, w, 1, {0: lag})

    thirds = {}

    def rs_pass(k, j):
        a, fixed = rs_fixed(k, j)
        b = rs_axes(k)[j + 1]
        rv, src = RV[j][k], P_[k]
        for w in range(2):
            rs_whole(k, j, w, 0).wait_recv()
        for o in ORDER:
            p, _ = near(b, o)
            for w, (sign, h1) in enumerate(WAYS):
                c1, dev = near(a, sign)
                where = view({**fixed, a: c1, b: p}, h1)
                got = rv_view(k, j, w, 0, {b: p})
                src[where] = (src[where].astype(f32) + rv[got].astype(f32)).astype(bf16)
                thirds[k, j, w, o] = remote(
                    src.at[where], rv.at[rv_view(k, j, w, 2, {b: p})],
                    rs_send.at[k, j, w, 2 + o], rs_recv.at[k, j, w, 2 + o], dev,
                )

    direct = {}

    def rs_close(k, j, o):
        a, fixed = rs_fixed(k, j)
        b = rs_axes(k)[j + 1]
        rv, src = RV[j][k], P_[k]
        p, dev = near(b, o)
        for w in range(2):
            thirds[k, j, w, o].wait_recv()
        for h in range(2):
            where = view({**fixed, a: me[a], b: p}, h)
            one = rv[rv_view(k, j, h, 2, {b: p})]
            two = rv[rv_view(k, j, 1 - h, 1, {b: p})]
            src[where] = (src[where].astype(f32) + one.astype(f32) + two.astype(f32)).astype(bf16)
        if j == 1:
            if o > 0:
                direct[k, o] = remote(
                    src.at[view({**fixed, a: me[a], b: p}, None)], RV[2][k].at[o - 1],
                    rd_send.at[k, o - 1], rd_recv.at[k, o - 1], dev,
                )
        elif o == 2:
            rs_open(k, 1, 0, 0)
            rs_open(k, 1, 1, 0)
        elif o == 1:
            rs_open(k, 1, 0, 1)
        elif o == 3:
            rs_open(k, 1, 1, 1)

    def turn(k):
        for c in range(4):
            sel = tuple(c if a == k else slice(None) for a in range(3)) + (slice(*(ROWS[k][0], sum(ROWS[k]))),)
            AT[k][c] = a2[sel].reshape(16 * ROWS[k][1], 256).T

    turn(2)
    rs_pass(0, 0)
    turn(0)
    rs_pass(2, 0)
    rs_pass(1, 0)
    turn(1)
    for j in range(2):
        if j > 0:
            for k in range(3):
                rs_pass(k, j)
        for k in range(3):
            for w in range(2):
                rs_whole(k, j, w, 1).wait_recv()
        for o in ORDER:
            for k in range(3):
                rs_close(k, j, o)
    for k, (lo, n) in enumerate(ROWS):
        for o in (1, 3, 2):
            direct[k, o].wait_recv()
        for h in range(2):
            total = P_[k][me[0], me[1], me[2], h].astype(f32)
            for o in range(3):
                total = total + RV[2][k][o, h].astype(f32)
            agg[lo : lo + n, pl.ds(pl.multiple_of(r * half + 128 * h, 128), 128)] = total.astype(bf16)

    mine = agg.at[:, cols]
    swap = remote(mine, mine, agg_send.at[0], agg_recv.at[0], (other, d))
    swap.wait_recv()
    pre = jnp.dot(agg[...], weight_ref[...], preferred_element_type=f32) + bias_ref[...]
    sig = jax.nn.sigmoid(pre)
    pg[...] = (cot_ref[...].astype(f32) * sig * (1.0 + pre * (1.0 - sig))).astype(bf16)
    actv[...] = (pre * sig).astype(bf16)
    row_grad = lax.dot_general(
        pg[...], weight_ref[cols, :], (((1,), (1,)), ((), ())), preferred_element_type=f32
    ).astype(bf16)
    for k, (lo, n) in enumerate(ROWS):
        for h in range(2):
            G_[k][me[0], me[1], me[2], h] = row_grad[lo : lo + n, 128 * h : 128 * h + 128]

    def ag_axes(k, j):
        axes = [(k + 2 - i) % 3 for i in range(3)]
        return axes[j], {axes[i]: me[axes[i]] for i in range(j + 1, 3)}

    near_block = {}

    def ag_direct(k):
        a, _ = ag_axes(k, 0)
        ref = G_[k].at[me]
        for o in (1, 3, 2):
            _, dev = near(a, o)
            near_block[k, o] = remote(ref, ref, ad_send.at[k, o - 1], ad_recv.at[k, o - 1], dev)

    moves = {}

    def ag_spot(k, j, o, origin, h):
        a, fixed = ag_axes(k, j)
        b, _ = ag_axes(k, j - 1)
        p, _ = near(b, o)
        return G_[k].at[view({**fixed, a: origin, b: p}, h)]

    def ag_open(k, j, o):
        a, _ = ag_axes(k, j)
        for m in range(2):
            for w, (sign, h1) in enumerate(WAYS):
                _, dev = near(a, sign)
                ref = ag_spot(k, j, o, me[a], h1 if m == 0 else 1 - h1)
                moves[k, j, o, w, m] = remote(
                    ref, ref, ag_send.at[k, j - 1, o, w, m], ag_recv.at[k, j - 1, o, w, m], dev
                )

    def ag_pass(k, j, o):
        a, _ = ag_axes(k, j)
        for w, (sign, h1) in enumerate(WAYS):
            _, dev = near(a, sign)
            origin, _ = near(a, 4 - sign)
            moves[k, j, o, w, 0].wait_recv()
            ref = ag_spot(k, j, o, origin, h1)
            moves[k, j, o, w, 2] = remote(
                ref, ref, ag_send.at[k, j - 1, o, w, 2], ag_recv.at[k, j - 1, o, w, 2], dev
            )

    def ag_wait(k, j, m):
        for o in range(4):
            for w in range(2):
                moves[k, j, o, w, m].wait_recv()

    WR = (wra, wrb, wrc)
    WS_AXES = (2, 0, 1)
    WA_AXES = (1, 0, 2)

    def wview(fixed):
        return tuple(fixed.get(a, slice(None)) for a in range(3))

    def ws_open(j):
        a = WS_AXES[j]
        fixed = {WS_AXES[i]: me[WS_AXES[i]] for i in range(j)}
        out = []
        for o in (1, 3, 2):
            c, dev = near(a, o)
            out.append(
                remote(wp.at[wview({**fixed, a: c})], WR[j].at[o - 1], ws_send.at[j, o - 1], ws_recv.at[j, o - 1], dev)
            )
        return out

    def ws_close(j, opened):
        for c in opened:
            c.wait_recv()
        where = wview({WS_AXES[i]: me[WS_AXES[i]] for i in range(j + 1)})
        total = wp[where].astype(f32)
        for o in range(3):
            total = total + WR[j][o].astype(f32)
        (wp if j < 2 else wg)[where] = total.astype(bf16)

    def wa_open(j):
        a = WA_AXES[j]
        fixed = {WA_AXES[i]: me[WA_AXES[i]] for i in range(j, 3)}
        ref = wg.at[wview(fixed)]
        out = []
        for o in (1, 3, 2):
            _, dev = near(a, o)
            out.append(remote(ref, ref, wa_send.at[j, o - 1], wa_recv.at[j, o - 1], dev))
        return out

    def wa_close(opened):
        for c in opened:
            c.wait_recv()

    for k in range(3):
        ag_direct(k)
    for k in range(3):
        ag_open(k, 1, 0)
    part = lax.dot_general(
        agg[...], pg[:, cols], (((0,), (0,)), ((), ())), preferred_element_type=f32
    ).astype(bf16)
    for h in range(2):
        wp[2 * h : 2 * h + 2] = part[:, 128 * h : 128 * h + 128].reshape(2, 4, 4, 16, 128)
    w = ws_open(0)
    act_ref[...] = actv[:, cols]
    acc[...] = jnp.zeros_like(acc)

    def backward(k, o):
        c, _ = near(k, o)
        n = 16 * ROWS[k][1]
        lhs = AT[k][c]
        for h in range(2):
            rhs = G_[k][view({k: c}, h)].reshape(n, 128)
            acc[:, 128 * h : 128 * h + 128] += jnp.dot(lhs, rhs, preferred_element_type=f32)

    for o in (1, 3):
        for k in range(3):
            near_block[k, o].wait_recv()
            ag_open(k, 1, 4 - o)
    for k in range(3):
        ag_pass(k, 1, 0)
    for k in range(3):
        near_block[k, 2].wait_recv()
        ag_open(k, 1, 2)
        ag_open(k, 2, 0)
    ws_close(0, w)
    w = ws_open(1)
    for o in (1, 3, 2):
        for k in range(3):
            ag_pass(k, 1, o)
    for k in range(3):
        ag_wait(k, 1, 1)
        ag_open(k, 2, 1)
        ag_open(k, 2, 3)
    ws_close(1, w)
    w = ws_open(2)
    for k in range(3):
        ag_wait(k, 1, 2)
        ag_open(k, 2, 2)
    for k in range(3):
        ag_pass(k, 2, 0)
    ws_close(2, w)
    w = wa_open(0)
    for k in range(3):
        backward(k, 0)
    for o in (1, 3):
        for k in range(3):
            ag_pass(k, 2, o)
    wa_close(w)
    w = wa_open(1)
    for k in range(3):
        ag_pass(k, 2, 2)
    wa_close(w)
    w = wa_open(2)
    for k in range(3):
        ag_wait(k, 2, 1)
        backward(k, 1)
        backward(k, 3)
    wa_close(w)
    for h in range(2):
        wsum_ref[:, 128 * h : 128 * h + 128] = wg[2 * h : 2 * h + 2].reshape(512, 128)
    for k in (2, 0, 1):
        ag_wait(k, 2, 2)
        backward(k, 2)
    fgrad_ref[...] = (acc[0:128, :] + acc[128:256, :]).astype(bf16)
    for c in started:
        c.wait_send()


def finish(act_in, wsum_in, fgrad_in, act_ref, wgrad_ref, fgrad_ref):
    act_ref[...] = act_in[...]
    fgrad_ref[...] = fgrad_in[...]
    wgrad_ref[...] = wsum_in[...].astype(jnp.float32) * (1.0 / math.sqrt(8192.0))


def layer(own, feat, weight, bias, cot):
    bf16, f32 = jnp.bfloat16, jnp.float32
    V = pltpu.VMEM
    dma = pltpu.SemaphoreType.DMA
    sizes = [n for _, n in ROWS]
    scratch = [V((4, 4, 4, 128, 256), bf16)]
    scratch += [V((4, 256, 16 * n), bf16) for n in sizes]
    scratch += [V((256, 256), bf16)]
    scratch += [V((4, 4, 4, 2, n, 128), bf16) for n in sizes]
    scratch += [V((4, 4, 4, 2, n, 128), bf16) for n in sizes]
    scratch += [V((2, 3, 4, 4, n, 128), bf16) for n in sizes]
    scratch += [V((2, 3, 4, n, 128), bf16) for n in sizes]
    scratch += [V((3, 2, n, 128), bf16) for n in sizes]
    scratch += [V((128, 512), bf16)] * 3
    scratch += [V((4, 4, 4, 16, 128), bf16)]
    scratch += [V((3, 4, 4, 16, 128), bf16), V((3, 4, 16, 128), bf16), V((3, 16, 128), bf16)]
    scratch += [V((4, 4, 4, 16, 128), bf16), V((256, 256), f32)]
    scratch += [dma((4,)), dma((4,)), dma((4,)), dma((1,)), dma((1,))]
    scratch += [dma((3, 2, 2, 6))] * 2 + [dma((3, 3))] * 4
    scratch += [dma((3, 2, 4, 2, 3))] * 2 + [dma((3, 3))] * 4
    whole = pl.BlockSpec(memory_space=pltpu.VMEM)
    return pl.pallas_call(
        layer_kernel,
        out_shape=[
            jax.ShapeDtypeStruct((128, 256), bf16),
            jax.ShapeDtypeStruct((512, 256), bf16),
            jax.ShapeDtypeStruct((128, 256), bf16),
        ],
        in_specs=[pl.BlockSpec(memory_space=pl.ANY)] + [whole] * 4,
        out_specs=[whole] * 3,
        scratch_shapes=scratch,
        compiler_params=pltpu.CompilerParams(collective_id=0, has_side_effects=True),
        name="layer",
    )(own, feat, weight, bias, cot)


def per_device(features, tiles, tile_dest, tile_count, weight, bias, cotangent):
    domains = lax.axis_size("dom")
    own = adjacency(tiles, tile_dest[:, 0], tile_count, domains)
    own = own.reshape(4, 4, 4, 128, 128)
    act, wsum, fgrad = layer(own, features, weight, bias.reshape(1, -1), cotangent)
    whole = pl.BlockSpec(memory_space=pltpu.VMEM)
    return pl.pallas_call(
        finish,
        out_shape=[
            jax.ShapeDtypeStruct(act.shape, act.dtype),
            jax.ShapeDtypeStruct(wsum.shape, jnp.float32),
            jax.ShapeDtypeStruct(fgrad.shape, fgrad.dtype),
        ],
        in_specs=[whole] * 3,
        out_specs=[whole] * 3,
        name="finish",
    )(act, wsum, fgrad)


def solution(mesh):
    in_specs = (
        P("dom", None),
        P(("rep", "dom"), None, None),
        P(("rep", "dom"), None),
        P(("rep", "dom")),
        P(),
        P(),
        P("dom", None),
    )
    out_specs = (P("dom", "rep"), P(None, "rep"), P("dom", "rep"))
    return jax.shard_map(
        per_device, mesh=mesh, in_specs=in_specs, out_specs=out_specs, check_vma=False
    )
```

```python
import math

import jax
import jax.numpy as jnp
from jax import lax
from jax.experimental import pallas as pl
from jax.experimental.pallas import tpu as pltpu
from jax.sharding import PartitionSpec as P


def index_tiles(dest_ref, count_ref, which_ref, share_ref, used):
    @pl.loop(0, used.shape[0], unroll=8)
    def _(b):
        used[b] = 0
        for k in range(2):
            which_ref[2 * b + k] = 0
            share_ref[2 * b + k] = 0

    @pl.loop(0, dest_ref.shape[0], unroll=8)
    def _(t):
        d = dest_ref[t]
        k = used[d]
        which_ref[2 * d + k] = t
        share_ref[2 * d + k] = jnp.maximum(count_ref[t], 1)
        used[d] = k + 1


def tile_index(dest, count, domains):
    smem = pl.BlockSpec(memory_space=pltpu.SMEM)
    shape = jax.ShapeDtypeStruct((2 * domains,), jnp.int32)
    return pl.pallas_call(
        index_tiles,
        out_shape=[shape, shape],
        in_specs=[smem, smem],
        out_specs=[smem, smem],
        scratch_shapes=[pltpu.SMEM((domains,), jnp.int32)],
        name="tile_index",
    )(dest, count)


ROWS = ((0, 48), (48, 48), (96, 32))
STRIDE = (16, 4, 1)
MESH = pl.DeviceIdType.MESH


def layer_kernel(
    which_ref, share_ref, tiles_ref, feat_ref, weight_ref, bias_ref, cot_ref,
    act_ref, wsum_ref, fgrad_ref,
    tv, a2, at0, at1, at2, ff, p0, p1, p2, g0, g1, g2,
    ra0, ra1, ra2, rb0, rb1, rb2, rc0, rc1, rc2,
    agg, pg, actv, wp, wra, wrb, wrc, wg, acc,
    own_sem, swap_send, swap_recv, agg_send, agg_recv,
    rs_send, rs_recv, rd_send, rd_recv, ad_send, ad_recv,
    ag_send, ag_recv, ws_send, ws_recv, wa_send, wa_recv,
):
    r = lax.axis_index("rep")
    d = lax.axis_index("dom")
    other = 1 - r
    me = (d // 16, (d // 4) % 4, d % 4)
    P_ = (p0, p1, p2)
    G_ = (g0, g1, g2)
    AT = (at0, at1, at2)
    RV = ((ra0, ra1, ra2), (rb0, rb1, rb2), (rc0, rc1, rc2))
    f32, bf16 = jnp.float32, jnp.bfloat16
    started = []

    def near(a, o):
        c = (me[a] + o) % 4
        return c, (r, d + (c - me[a]) * STRIDE[a])

    barrier = pltpu.get_barrier_semaphore()
    pl.semaphore_signal(barrier, inc=1, device_id=(other, d), device_id_type=MESH)
    for a in range(3):
        for o in (1, 2, 3):
            pl.semaphore_signal(barrier, inc=1, device_id=near(a, o)[1], device_id_type=MESH)
    load = pltpu.make_async_copy(tiles_ref, tv, own_sem.at[0])
    load.start()
    half = 256
    cols = pl.ds(pl.multiple_of(r * half, half), half)
    ff[0:128, :] = feat_ref[:, cols]
    ff[128:256, :] = feat_ref[:, cols]
    load.wait()

    def build(y, _):
        for x in range(4):
            b = 4 * y + x
            total = jnp.zeros((128, 128), f32)
            for k in range(2):
                t = which_ref[2 * b + k]
                c = jnp.full((8, 128), share_ref[2 * b + k], jnp.int32).astype(f32)
                scale = jnp.where(c > 0.0, lax.rsqrt(jnp.maximum(c, 1.0)), 0.0)[0:1, :]
                total = total + tv[t].astype(f32) * scale
            a2[y // 4, y % 4, x, :, 0:128] = total.astype(bf16)
        return 0

    lax.fori_loop(0, 16, build, 0)
    pl.semaphore_wait(barrier, 10)

    def remote(src, dst, ssem, rsem, dev):
        c = pltpu.make_async_remote_copy(
            src_ref=src, dst_ref=dst, send_sem=ssem, recv_sem=rsem,
            device_id=dev, device_id_type=MESH,
        )
        c.start()
        started.append(c)
        return c

    ORDER = (2, 1, 3, 0)
    WAYS = ((1, 0), (3, 1))
    swaps = []
    for s, o in enumerate(ORDER):
        i, _ = near(0, o)
        swaps.append(
            remote(
                a2.at[i, :, :, :, 0:128], a2.at[i, :, :, :, 128:256],
                swap_send.at[s], swap_recv.at[s], (other, d),
            )
        )

    def view(fixed, h):
        return tuple(fixed.get(a, slice(None)) for a in range(3)) + ((h,) if h is not None else ())

    def rs_axes(k):
        return [(k + i) % 3 for i in range(3)]

    def rs_fixed(k, j):
        axes = rs_axes(k)
        return axes[j], {axes[i]: me[axes[i]] for i in range(j)}

    def rs_send_of(k, j, w, m, extra):
        a, fixed = rs_fixed(k, j)
        sign, h1 = WAYS[w]
        c, _ = near(a, 2 if m == 0 else sign)
        _, dev = near(a, sign)
        h = h1 if m == 0 else 1 - h1
        spot = rv_view(k, j, w, m, extra)
        return dict(
            src_ref=P_[k].at[view({**fixed, a: c, **extra}, h)], dst_ref=RV[j][k].at[spot],
            send_sem=rs_send.at[k, j, w, m], recv_sem=rs_recv.at[k, j, w, m],
            device_id=dev, device_id_type=MESH,
        )

    def rv_view(k, j, w, m, extra):
        a, fixed = rs_fixed(k, j)
        left = [x for x in range(3) if x != a and x not in fixed]
        return (w, m) + tuple(extra.get(x, slice(None)) for x in left)

    def rs_open(k, j, w, m, extra=None):
        pltpu.make_async_remote_copy(**rs_send_of(k, j, w, m, extra or {})).start()

    def rs_whole(k, j, w, m):
        c = pltpu.make_async_remote_copy(**rs_send_of(k, j, w, m, {}))
        started.append(c)
        return c

    lag = None
    for s, o in enumerate(ORDER):
        i, _ = near(0, o)
        swaps[s].wait_recv()

        def forward(j, _, i=i):
            lhs = a2[i, j].reshape(512, 256)
            res = jnp.dot(lhs, ff[...], preferred_element_type=f32).astype(bf16)
            res = res.reshape(4, 128, 256)
            for k, (lo, n) in enumerate(ROWS):
                for h in range(2):
                    P_[k][i, j, :, h] = res[:, lo : lo + n, 128 * h : 128 * h + 128]
            return 0

        lax.fori_loop(0, 4, forward, 0)
        if o == 2:
            rs_open(0, 0, 0, 0)
            rs_open(0, 0, 1, 0)
        elif o == 1:
            rs_open(0, 0, 0, 1)
        elif o == 3:
            rs_open(0, 0, 1, 1)
        for k in (1, 2):
            for w in range(2):
                rs_open(k, 0, w, 0, {0: i})
        for k in (1, 2):
            for w in range(2):
                if lag is not None:
                    rs_open(k, 0, w, 1, {0: lag})
        lag = i
    for k in (1, 2):
        for w in range(2):
            rs_open(k, 0, w, 1, {0: lag})

    thirds = {}

    def rs_pass(k, j):
        a, fixed = rs_fixed(k, j)
        b = rs_axes(k)[j + 1]
        rv, src = RV[j][k], P_[k]
        for w in range(2):
            rs_whole(k, j, w, 0).wait_recv()
        for o in ORDER:
            p, _ = near(b, o)
            for w, (sign, h1) in enumerate(WAYS):
                c1, dev = near(a, sign)
                where = view({**fixed, a: c1, b: p}, h1)
                got = rv_view(k, j, w, 0, {b: p})
                src[where] = (src[where].astype(f32) + rv[got].astype(f32)).astype(bf16)
                thirds[k, j, w, o] = remote(
                    src.at[where], rv.at[rv_view(k, j, w, 2, {b: p})],
                    rs_send.at[k, j, w, 2 + o], rs_recv.at[k, j, w, 2 + o], dev,
                )

    direct = {}

    def rs_close(k, j, o):
        a, fixed = rs_fixed(k, j)
        b = rs_axes(k)[j + 1]
        rv, src = RV[j][k], P_[k]
        p, dev = near(b, o)
        for w in range(2):
            thirds[k, j, w, o].wait_recv()
        for h in range(2):
            where = view({**fixed, a: me[a], b: p}, h)
            one = rv[rv_view(k, j, h, 2, {b: p})]
            two = rv[rv_view(k, j, 1 - h, 1, {b: p})]
            src[where] = (src[where].astype(f32) + one.astype(f32) + two.astype(f32)).astype(bf16)
        if j == 1:
            if o > 0:
                direct[k, o] = remote(
                    src.at[view({**fixed, a: me[a], b: p}, None)], RV[2][k].at[o - 1],
                    rd_send.at[k, o - 1], rd_recv.at[k, o - 1], dev,
                )
        elif o == 2:
            rs_open(k, 1, 0, 0)
            rs_open(k, 1, 1, 0)
        elif o == 1:
            rs_open(k, 1, 0, 1)
        elif o == 3:
            rs_open(k, 1, 1, 1)

    def turn(k):
        for c in range(4):
            sel = tuple(c if a == k else slice(None) for a in range(3)) + (slice(*(ROWS[k][0], sum(ROWS[k]))),)
            AT[k][c] = a2[sel].reshape(16 * ROWS[k][1], 256).T

    turn(2)
    rs_pass(0, 0)
    turn(0)
    rs_pass(2, 0)
    rs_pass(1, 0)
    turn(1)
    for j in range(2):
        if j > 0:
            for k in range(3):
                rs_pass(k, j)
        for k in range(3):
            for w in range(2):
                rs_whole(k, j, w, 1).wait_recv()
        for o in ORDER:
            for k in range(3):
                rs_close(k, j, o)
    for k, (lo, n) in enumerate(ROWS):
        for o in (1, 3, 2):
            direct[k, o].wait_recv()
        for h in range(2):
            total = P_[k][me[0], me[1], me[2], h].astype(f32)
            for o in range(3):
                total = total + RV[2][k][o, h].astype(f32)
            agg[lo : lo + n, pl.ds(pl.multiple_of(r * half + 128 * h, 128), 128)] = total.astype(bf16)

    mine = agg.at[:, cols]
    swap = remote(mine, mine, agg_send.at[0], agg_recv.at[0], (other, d))
    swap.wait_recv()
    pre = jnp.dot(agg[...], weight_ref[...], preferred_element_type=f32) + bias_ref[...]
    sig = jax.nn.sigmoid(pre)
    pg[...] = (cot_ref[...].astype(f32) * sig * (1.0 + pre * (1.0 - sig))).astype(bf16)
    actv[...] = (pre * sig).astype(bf16)
    row_grad = lax.dot_general(
        pg[...], weight_ref[cols, :], (((1,), (1,)), ((), ())), preferred_element_type=f32
    ).astype(bf16)
    for k, (lo, n) in enumerate(ROWS):
        for h in range(2):
            G_[k][me[0], me[1], me[2], h] = row_grad[lo : lo + n, 128 * h : 128 * h + 128]

    def ag_axes(k, j):
        axes = [(k + 2 - i) % 3 for i in range(3)]
        return axes[j], {axes[i]: me[axes[i]] for i in range(j + 1, 3)}

    near_block = {}

    def ag_direct(k):
        a, _ = ag_axes(k, 0)
        ref = G_[k].at[me]
        for o in (1, 3, 2):
            _, dev = near(a, o)
            near_block[k, o] = remote(ref, ref, ad_send.at[k, o - 1], ad_recv.at[k, o - 1], dev)

    moves = {}

    def ag_spot(k, j, o, origin, h):
        a, fixed = ag_axes(k, j)
        b, _ = ag_axes(k, j - 1)
        p, _ = near(b, o)
        return G_[k].at[view({**fixed, a: origin, b: p}, h)]

    def ag_open(k, j, o):
        a, _ = ag_axes(k, j)
        for m in range(2):
            for w, (sign, h1) in enumerate(WAYS):
                _, dev = near(a, sign)
                ref = ag_spot(k, j, o, me[a], h1 if m == 0 else 1 - h1)
                moves[k, j, o, w, m] = remote(
                    ref, ref, ag_send.at[k, j - 1, o, w, m], ag_recv.at[k, j - 1, o, w, m], dev
                )

    def ag_pass(k, j, o):
        a, _ = ag_axes(k, j)
        for w, (sign, h1) in enumerate(WAYS):
            _, dev = near(a, sign)
            origin, _ = near(a, 4 - sign)
            moves[k, j, o, w, 0].wait_recv()
            ref = ag_spot(k, j, o, origin, h1)
            moves[k, j, o, w, 2] = remote(
                ref, ref, ag_send.at[k, j - 1, o, w, 2], ag_recv.at[k, j - 1, o, w, 2], dev
            )

    def ag_wait(k, j, m):
        for o in range(4):
            for w in range(2):
                moves[k, j, o, w, m].wait_recv()

    WR = (wra, wrb, wrc)
    WS_AXES = (2, 0, 1)
    WA_AXES = (1, 0, 2)

    def wview(fixed):
        return tuple(fixed.get(a, slice(None)) for a in range(3))

    def ws_open(j):
        a = WS_AXES[j]
        fixed = {WS_AXES[i]: me[WS_AXES[i]] for i in range(j)}
        out = []
        for o in (1, 3, 2):
            c, dev = near(a, o)
            out.append(
                remote(wp.at[wview({**fixed, a: c})], WR[j].at[o - 1], ws_send.at[j, o - 1], ws_recv.at[j, o - 1], dev)
            )
        return out

    def ws_close(j, opened):
        for c in opened:
            c.wait_recv()
        where = wview({WS_AXES[i]: me[WS_AXES[i]] for i in range(j + 1)})
        total = wp[where].astype(f32)
        for o in range(3):
            total = total + WR[j][o].astype(f32)
        (wp if j < 2 else wg)[where] = total.astype(bf16)

    def wa_open(j):
        a = WA_AXES[j]
        fixed = {WA_AXES[i]: me[WA_AXES[i]] for i in range(j, 3)}
        ref = wg.at[wview(fixed)]
        out = []
        for o in (1, 3, 2):
            _, dev = near(a, o)
            out.append(remote(ref, ref, wa_send.at[j, o - 1], wa_recv.at[j, o - 1], dev))
        return out

    def wa_close(opened):
        for c in opened:
            c.wait_recv()

    for k in range(3):
        ag_direct(k)
    for k in range(3):
        ag_open(k, 1, 0)
    part = lax.dot_general(
        agg[...], pg[:, cols], (((0,), (0,)), ((), ())), preferred_element_type=f32
    ).astype(bf16)
    for h in range(2):
        wp[2 * h : 2 * h + 2] = part[:, 128 * h : 128 * h + 128].reshape(2, 4, 4, 16, 128)
    w = ws_open(0)
    act_ref[...] = actv[:, cols]
    acc[...] = jnp.zeros_like(acc)

    def backward(k, o):
        c, _ = near(k, o)
        n = 16 * ROWS[k][1]
        lhs = AT[k][c]
        for h in range(2):
            rhs = G_[k][view({k: c}, h)].reshape(n, 128)
            acc[:, 128 * h : 128 * h + 128] += jnp.dot(lhs, rhs, preferred_element_type=f32)

    for o in (1, 3):
        for k in range(3):
            near_block[k, o].wait_recv()
            ag_open(k, 1, 4 - o)
    for k in range(3):
        ag_pass(k, 1, 0)
    for k in range(3):
        near_block[k, 2].wait_recv()
        ag_open(k, 1, 2)
        ag_open(k, 2, 0)
    ws_close(0, w)
    w = ws_open(1)
    for o in (1, 3, 2):
        for k in range(3):
            ag_pass(k, 1, o)
    for k in range(3):
        ag_wait(k, 1, 1)
        ag_open(k, 2, 1)
        ag_open(k, 2, 3)
    ws_close(1, w)
    w = ws_open(2)
    for k in range(3):
        ag_wait(k, 1, 2)
        ag_open(k, 2, 2)
    for k in range(3):
        ag_pass(k, 2, 0)
    ws_close(2, w)
    w = wa_open(0)
    for k in range(3):
        backward(k, 0)
    for o in (1, 3):
        for k in range(3):
            ag_pass(k, 2, o)
    wa_close(w)
    w = wa_open(1)
    for k in range(3):
        ag_pass(k, 2, 2)
    wa_close(w)
    w = wa_open(2)
    for k in range(3):
        ag_wait(k, 2, 1)
        backward(k, 1)
        backward(k, 3)
    wa_close(w)
    for h in range(2):
        wsum_ref[:, 128 * h : 128 * h + 128] = wg[2 * h : 2 * h + 2].reshape(512, 128)
    for k in (2, 0, 1):
        ag_wait(k, 2, 2)
        backward(k, 2)
    fgrad_ref[...] = (acc[0:128, :] + acc[128:256, :]).astype(bf16)
    for c in started:
        c.wait_send()


def finish(act_in, wsum_in, fgrad_in, act_ref, wgrad_ref, fgrad_ref):
    act_ref[...] = act_in[...]
    fgrad_ref[...] = fgrad_in[...]
    wgrad_ref[...] = wsum_in[...].astype(jnp.float32) * (1.0 / math.sqrt(8192.0))


def layer(which, share, tiles, feat, weight, bias, cot):
    bf16, f32 = jnp.bfloat16, jnp.float32
    V = pltpu.VMEM
    dma = pltpu.SemaphoreType.DMA
    sizes = [n for _, n in ROWS]
    scratch = [V(tiles.shape, bf16), V((4, 4, 4, 128, 256), bf16)]
    scratch += [V((4, 256, 16 * n), bf16) for n in sizes]
    scratch += [V((256, 256), bf16)]
    scratch += [V((4, 4, 4, 2, n, 128), bf16) for n in sizes]
    scratch += [V((4, 4, 4, 2, n, 128), bf16) for n in sizes]
    scratch += [V((2, 3, 4, 4, n, 128), bf16) for n in sizes]
    scratch += [V((2, 3, 4, n, 128), bf16) for n in sizes]
    scratch += [V((3, 2, n, 128), bf16) for n in sizes]
    scratch += [V((128, 512), bf16)] * 3
    scratch += [V((4, 4, 4, 16, 128), bf16)]
    scratch += [V((3, 4, 4, 16, 128), bf16), V((3, 4, 16, 128), bf16), V((3, 16, 128), bf16)]
    scratch += [V((4, 4, 4, 16, 128), bf16), V((256, 256), f32)]
    scratch += [dma((1,)), dma((4,)), dma((4,)), dma((1,)), dma((1,))]
    scratch += [dma((3, 2, 2, 6))] * 2 + [dma((3, 3))] * 4
    scratch += [dma((3, 2, 4, 2, 3))] * 2 + [dma((3, 3))] * 4
    whole = pl.BlockSpec(memory_space=pltpu.VMEM)
    return pl.pallas_call(
        layer_kernel,
        out_shape=[
            jax.ShapeDtypeStruct((128, 256), bf16),
            jax.ShapeDtypeStruct((512, 256), bf16),
            jax.ShapeDtypeStruct((128, 256), bf16),
        ],
        in_specs=[pl.BlockSpec(memory_space=pltpu.SMEM)] * 2 + [pl.BlockSpec(memory_space=pl.ANY)] + [whole] * 4,
        out_specs=[whole] * 3,
        scratch_shapes=scratch,
        compiler_params=pltpu.CompilerParams(collective_id=0, has_side_effects=True),
        name="layer",
    )(which, share, tiles, feat, weight, bias, cot)


def per_device(features, tiles, tile_dest, tile_count, weight, bias, cotangent):
    domains = lax.axis_size("dom")
    which, share = tile_index(tile_dest[:, 0], tile_count, domains)
    act, wsum, fgrad = layer(which, share, tiles, features, weight, bias.reshape(1, -1), cotangent)
    whole = pl.BlockSpec(memory_space=pltpu.VMEM)
    return pl.pallas_call(
        finish,
        out_shape=[
            jax.ShapeDtypeStruct(act.shape, act.dtype),
            jax.ShapeDtypeStruct(wsum.shape, jnp.float32),
            jax.ShapeDtypeStruct(fgrad.shape, fgrad.dtype),
        ],
        in_specs=[whole] * 3,
        out_specs=[whole] * 3,
        name="finish",
    )(act, wsum, fgrad)


def solution(mesh):
    in_specs = (
        P("dom", None),
        P(("rep", "dom"), None, None),
        P(("rep", "dom"), None),
        P(("rep", "dom")),
        P(),
        P(),
        P("dom", None),
    )
    out_specs = (P("dom", "rep"), P(None, "rep"), P("dom", "rep"))
    return jax.shard_map(
        per_device, mesh=mesh, in_specs=in_specs, out_specs=out_specs, check_vma=False
    )
```

```python
import math

import jax
import jax.numpy as jnp
from jax import lax
from jax.experimental import pallas as pl
from jax.experimental.pallas import tpu as pltpu
from jax.sharding import PartitionSpec as P


def index_tiles(dest_ref, count_ref, which_ref, share_ref, used):
    @pl.loop(0, used.shape[0], unroll=8)
    def _(b):
        used[b] = 0
        for k in range(2):
            which_ref[2 * b + k] = 0
            share_ref[2 * b + k] = 0

    @pl.loop(0, dest_ref.shape[0], unroll=8)
    def _(t):
        d = dest_ref[t]
        k = used[d]
        which_ref[2 * d + k] = t
        share_ref[2 * d + k] = jnp.maximum(count_ref[t], 1)
        used[d] = k + 1


def tile_index(dest, count, domains):
    smem = pl.BlockSpec(memory_space=pltpu.SMEM)
    shape = jax.ShapeDtypeStruct((2 * domains,), jnp.int32)
    return pl.pallas_call(
        index_tiles,
        out_shape=[shape, shape],
        in_specs=[smem, smem],
        out_specs=[smem, smem],
        scratch_shapes=[pltpu.SMEM((domains,), jnp.int32)],
        name="tile_index",
    )(dest, count)


ROWS = ((0, 48), (48, 40), (88, 40))
STRIDE = (16, 4, 1)
MESH = pl.DeviceIdType.MESH


def layer_kernel(
    which_ref, share_ref, tiles_ref, feat_ref, weight_ref, bias_ref, cot_ref,
    act_ref, wsum_ref, fgrad_ref,
    tv, a2, at0, at1, at2, ff, p0, p1, p2, g0, g1, g2,
    ra0, ra1, ra2, rb0, rb1, rb2, rc0, rc1, rc2,
    agg, pg, actv, wp, wra, wrb, wrc, wg, acc,
    own_sem, swap_send, swap_recv, agg_send, agg_recv,
    rs_send, rs_recv, rd_send, rd_recv, ad_send, ad_recv,
    ag_send, ag_recv, ws_send, ws_recv, wa_send, wa_recv,
):
    r = lax.axis_index("rep")
    d = lax.axis_index("dom")
    other = 1 - r
    me = (d // 16, (d // 4) % 4, d % 4)
    P_ = (p0, p1, p2)
    G_ = (g0, g1, g2)
    AT = (at0, at1, at2)
    RV = ((ra0, ra1, ra2), (rb0, rb1, rb2), (rc0, rc1, rc2))
    f32, bf16 = jnp.float32, jnp.bfloat16
    started = []

    def near(a, o):
        c = (me[a] + o) % 4
        return c, (r, d + (c - me[a]) * STRIDE[a])

    barrier = pltpu.get_barrier_semaphore()
    pl.semaphore_signal(barrier, inc=1, device_id=(other, d), device_id_type=MESH)
    for a in range(3):
        for o in (1, 2, 3):
            pl.semaphore_signal(barrier, inc=1, device_id=near(a, o)[1], device_id_type=MESH)
    load = pltpu.make_async_copy(tiles_ref, tv, own_sem.at[0])
    load.start()
    half = 256
    cols = pl.ds(pl.multiple_of(r * half, half), half)
    ff[0:128, :] = feat_ref[:, cols]
    ff[128:256, :] = feat_ref[:, cols]
    load.wait()

    def build(y, _):
        for x in range(4):
            b = 4 * y + x
            total = jnp.zeros((128, 128), f32)
            for k in range(2):
                t = which_ref[2 * b + k]
                c = jnp.full((8, 128), share_ref[2 * b + k], jnp.int32).astype(f32)
                scale = jnp.where(c > 0.0, lax.rsqrt(jnp.maximum(c, 1.0)), 0.0)[0:1, :]
                total = total + tv[t].astype(f32) * scale
            a2[y // 4, y % 4, x, :, 0:128] = total.astype(bf16)
        return 0

    lax.fori_loop(0, 16, build, 0)
    pl.semaphore_wait(barrier, 10)

    def remote(src, dst, ssem, rsem, dev):
        c = pltpu.make_async_remote_copy(
            src_ref=src, dst_ref=dst, send_sem=ssem, recv_sem=rsem,
            device_id=dev, device_id_type=MESH,
        )
        c.start()
        started.append(c)
        return c

    ORDER = (2, 1, 3, 0)
    WAYS = ((1, 0), (3, 1))
    swaps = []
    for s, o in enumerate(ORDER):
        i, _ = near(0, o)
        swaps.append(
            remote(
                a2.at[i, :, :, :, 0:128], a2.at[i, :, :, :, 128:256],
                swap_send.at[s], swap_recv.at[s], (other, d),
            )
        )

    def view(fixed, h):
        return tuple(fixed.get(a, slice(None)) for a in range(3)) + ((h,) if h is not None else ())

    def rs_axes(k):
        return [(k + i) % 3 for i in range(3)]

    def rs_fixed(k, j):
        axes = rs_axes(k)
        return axes[j], {axes[i]: me[axes[i]] for i in range(j)}

    def rs_send_of(k, j, w, m, extra):
        a, fixed = rs_fixed(k, j)
        sign, h1 = WAYS[w]
        c, _ = near(a, 2 if m == 0 else sign)
        _, dev = near(a, sign)
        h = h1 if m == 0 else 1 - h1
        spot = rv_view(k, j, w, m, extra)
        return dict(
            src_ref=P_[k].at[view({**fixed, a: c, **extra}, h)], dst_ref=RV[j][k].at[spot],
            send_sem=rs_send.at[k, j, w, m], recv_sem=rs_recv.at[k, j, w, m],
            device_id=dev, device_id_type=MESH,
        )

    def rv_view(k, j, w, m, extra):
        a, fixed = rs_fixed(k, j)
        left = [x for x in range(3) if x != a and x not in fixed]
        return (w, m) + tuple(extra.get(x, slice(None)) for x in left)

    def rs_open(k, j, w, m, extra=None):
        pltpu.make_async_remote_copy(**rs_send_of(k, j, w, m, extra or {})).start()

    def rs_whole(k, j, w, m):
        c = pltpu.make_async_remote_copy(**rs_send_of(k, j, w, m, {}))
        started.append(c)
        return c

    lag = None
    for s, o in enumerate(ORDER):
        i, _ = near(0, o)
        swaps[s].wait_recv()

        def forward(j, _, i=i):
            lhs = a2[i, j].reshape(512, 256)
            res = jnp.dot(lhs, ff[...], preferred_element_type=f32).astype(bf16)
            res = res.reshape(4, 128, 256)
            for k, (lo, n) in enumerate(ROWS):
                for h in range(2):
                    P_[k][i, j, :, h] = res[:, lo : lo + n, 128 * h : 128 * h + 128]
            return 0

        lax.fori_loop(0, 4, forward, 0)
        if o == 2:
            rs_open(0, 0, 0, 0)
            rs_open(0, 0, 1, 0)
        elif o == 1:
            rs_open(0, 0, 0, 1)
        elif o == 3:
            rs_open(0, 0, 1, 1)
        for k in (1, 2):
            for w in range(2):
                rs_open(k, 0, w, 0, {0: i})
        for k in (1, 2):
            for w in range(2):
                if lag is not None:
                    rs_open(k, 0, w, 1, {0: lag})
        lag = i
    for k in (1, 2):
        for w in range(2):
            rs_open(k, 0, w, 1, {0: lag})

    thirds = {}

    def rs_pass(k, j):
        a, fixed = rs_fixed(k, j)
        b = rs_axes(k)[j + 1]
        rv, src = RV[j][k], P_[k]
        for w in range(2):
            rs_whole(k, j, w, 0).wait_recv()
        for o in ORDER:
            p, _ = near(b, o)
            for w, (sign, h1) in enumerate(WAYS):
                c1, dev = near(a, sign)
                where = view({**fixed, a: c1, b: p}, h1)
                got = rv_view(k, j, w, 0, {b: p})
                src[where] = (src[where].astype(f32) + rv[got].astype(f32)).astype(bf16)
                thirds[k, j, w, o] = remote(
                    src.at[where], rv.at[rv_view(k, j, w, 2, {b: p})],
                    rs_send.at[k, j, w, 2 + o], rs_recv.at[k, j, w, 2 + o], dev,
                )

    direct = {}

    def rs_close(k, j, o):
        a, fixed = rs_fixed(k, j)
        b = rs_axes(k)[j + 1]
        rv, src = RV[j][k], P_[k]
        p, dev = near(b, o)
        for w in range(2):
            thirds[k, j, w, o].wait_recv()
        for h in range(2):
            where = view({**fixed, a: me[a], b: p}, h)
            one = rv[rv_view(k, j, h, 2, {b: p})]
            two = rv[rv_view(k, j, 1 - h, 1, {b: p})]
            src[where] = (src[where].astype(f32) + one.astype(f32) + two.astype(f32)).astype(bf16)
        if j == 1:
            if o > 0:
                direct[k, o] = remote(
                    src.at[view({**fixed, a: me[a], b: p}, None)], RV[2][k].at[o - 1],
                    rd_send.at[k, o - 1], rd_recv.at[k, o - 1], dev,
                )
        elif o == 2:
            rs_open(k, 1, 0, 0)
            rs_open(k, 1, 1, 0)
        elif o == 1:
            rs_open(k, 1, 0, 1)
        elif o == 3:
            rs_open(k, 1, 1, 1)

    def turn(k):
        for c in range(4):
            sel = tuple(c if a == k else slice(None) for a in range(3)) + (slice(*(ROWS[k][0], sum(ROWS[k]))),)
            AT[k][c] = a2[sel].reshape(16 * ROWS[k][1], 256).T

    turn(2)
    rs_pass(0, 0)
    turn(0)
    rs_pass(2, 0)
    rs_pass(1, 0)
    turn(1)
    for j in range(2):
        if j > 0:
            for k in range(3):
                rs_pass(k, j)
        for k in range(3):
            for w in range(2):
                rs_whole(k, j, w, 1).wait_recv()
        for o in ORDER:
            for k in range(3):
                rs_close(k, j, o)
    for k, (lo, n) in enumerate(ROWS):
        for o in (1, 3, 2):
            direct[k, o].wait_recv()
        for h in range(2):
            total = P_[k][me[0], me[1], me[2], h].astype(f32)
            for o in range(3):
                total = total + RV[2][k][o, h].astype(f32)
            agg[lo : lo + n, pl.ds(pl.multiple_of(r * half + 128 * h, 128), 128)] = total.astype(bf16)

    mine = agg.at[:, cols]
    swap = remote(mine, mine, agg_send.at[0], agg_recv.at[0], (other, d))
    swap.wait_recv()
    pre = jnp.dot(agg[...], weight_ref[...], preferred_element_type=f32) + bias_ref[...]
    sig = jax.nn.sigmoid(pre)
    pg[...] = (cot_ref[...].astype(f32) * sig * (1.0 + pre * (1.0 - sig))).astype(bf16)
    actv[...] = (pre * sig).astype(bf16)
    row_grad = lax.dot_general(
        pg[...], weight_ref[cols, :], (((1,), (1,)), ((), ())), preferred_element_type=f32
    ).astype(bf16)
    for k, (lo, n) in enumerate(ROWS):
        for h in range(2):
            G_[k][me[0], me[1], me[2], h] = row_grad[lo : lo + n, 128 * h : 128 * h + 128]

    def ag_axes(k, j):
        axes = [(k + 2 - i) % 3 for i in range(3)]
        return axes[j], {axes[i]: me[axes[i]] for i in range(j + 1, 3)}

    near_block = {}

    def ag_direct(k):
        a, _ = ag_axes(k, 0)
        ref = G_[k].at[me]
        for o in (1, 3, 2):
            _, dev = near(a, o)
            near_block[k, o] = remote(ref, ref, ad_send.at[k, o - 1], ad_recv.at[k, o - 1], dev)

    moves = {}

    def ag_spot(k, j, o, origin, h):
        a, fixed = ag_axes(k, j)
        b, _ = ag_axes(k, j - 1)
        p, _ = near(b, o)
        return G_[k].at[view({**fixed, a: origin, b: p}, h)]

    def ag_open(k, j, o):
        a, _ = ag_axes(k, j)
        for m in range(2):
            for w, (sign, h1) in enumerate(WAYS):
                _, dev = near(a, sign)
                ref = ag_spot(k, j, o, me[a], h1 if m == 0 else 1 - h1)
                moves[k, j, o, w, m] = remote(
                    ref, ref, ag_send.at[k, j - 1, o, w, m], ag_recv.at[k, j - 1, o, w, m], dev
                )

    def ag_pass(k, j, o):
        a, _ = ag_axes(k, j)
        for w, (sign, h1) in enumerate(WAYS):
            _, dev = near(a, sign)
            origin, _ = near(a, 4 - sign)
            moves[k, j, o, w, 0].wait_recv()
            ref = ag_spot(k, j, o, origin, h1)
            moves[k, j, o, w, 2] = remote(
                ref, ref, ag_send.at[k, j - 1, o, w, 2], ag_recv.at[k, j - 1, o, w, 2], dev
            )

    def ag_wait(k, j, m):
        for o in range(4):
            for w in range(2):
                moves[k, j, o, w, m].wait_recv()

    WR = (wra, wrb, wrc)
    WS_AXES = (2, 0, 1)
    WA_AXES = (1, 0, 2)

    def wview(fixed):
        return tuple(fixed.get(a, slice(None)) for a in range(3))

    def ws_open(j):
        a = WS_AXES[j]
        fixed = {WS_AXES[i]: me[WS_AXES[i]] for i in range(j)}
        out = []
        for o in (1, 3, 2):
            c, dev = near(a, o)
            out.append(
                remote(wp.at[wview({**fixed, a: c})], WR[j].at[o - 1], ws_send.at[j, o - 1], ws_recv.at[j, o - 1], dev)
            )
        return out

    def ws_close(j, opened):
        for c in opened:
            c.wait_recv()
        where = wview({WS_AXES[i]: me[WS_AXES[i]] for i in range(j + 1)})
        total = wp[where].astype(f32)
        for o in range(3):
            total = total + WR[j][o].astype(f32)
        (wp if j < 2 else wg)[where] = total.astype(bf16)

    def wa_open(j):
        a = WA_AXES[j]
        fixed = {WA_AXES[i]: me[WA_AXES[i]] for i in range(j, 3)}
        ref = wg.at[wview(fixed)]
        out = []
        for o in (1, 3, 2):
            _, dev = near(a, o)
            out.append(remote(ref, ref, wa_send.at[j, o - 1], wa_recv.at[j, o - 1], dev))
        return out

    def wa_close(opened):
        for c in opened:
            c.wait_recv()

    for k in range(3):
        ag_direct(k)
    for k in range(3):
        ag_open(k, 1, 0)
    part = lax.dot_general(
        agg[...], pg[:, cols], (((0,), (0,)), ((), ())), preferred_element_type=f32
    ).astype(bf16)
    for h in range(2):
        wp[2 * h : 2 * h + 2] = part[:, 128 * h : 128 * h + 128].reshape(2, 4, 4, 16, 128)
    w = ws_open(0)
    act_ref[...] = actv[:, cols]
    acc[...] = jnp.zeros_like(acc)

    def backward(k, o):
        c, _ = near(k, o)
        n = 16 * ROWS[k][1]
        lhs = AT[k][c]
        for h in range(2):
            rhs = G_[k][view({k: c}, h)].reshape(n, 128)
            acc[:, 128 * h : 128 * h + 128] += jnp.dot(lhs, rhs, preferred_element_type=f32)

    for o in (1, 3):
        for k in range(3):
            near_block[k, o].wait_recv()
            ag_open(k, 1, 4 - o)
    for k in range(3):
        ag_pass(k, 1, 0)
    for k in range(3):
        near_block[k, 2].wait_recv()
        ag_open(k, 1, 2)
        ag_open(k, 2, 0)
    ws_close(0, w)
    w = ws_open(1)
    for o in (1, 3, 2):
        for k in range(3):
            ag_pass(k, 1, o)
    for k in range(3):
        ag_wait(k, 1, 1)
        ag_open(k, 2, 1)
        ag_open(k, 2, 3)
    ws_close(1, w)
    w = ws_open(2)
    for k in range(3):
        ag_wait(k, 1, 2)
        ag_open(k, 2, 2)
    for k in range(3):
        ag_pass(k, 2, 0)
    ws_close(2, w)
    w = wa_open(0)
    for k in range(3):
        backward(k, 0)
    for o in (1, 3):
        for k in range(3):
            ag_pass(k, 2, o)
    wa_close(w)
    w = wa_open(1)
    for k in range(3):
        ag_pass(k, 2, 2)
    wa_close(w)
    w = wa_open(2)
    for k in range(3):
        ag_wait(k, 2, 1)
        backward(k, 1)
        backward(k, 3)
    wa_close(w)
    for h in range(2):
        wsum_ref[:, 128 * h : 128 * h + 128] = wg[2 * h : 2 * h + 2].reshape(512, 128)
    for k in (2, 0, 1):
        ag_wait(k, 2, 2)
        backward(k, 2)
    fgrad_ref[...] = (acc[0:128, :] + acc[128:256, :]).astype(bf16)
    for c in started:
        c.wait_send()


def finish(act_in, wsum_in, fgrad_in, act_ref, wgrad_ref, fgrad_ref):
    act_ref[...] = act_in[...]
    fgrad_ref[...] = fgrad_in[...]
    wgrad_ref[...] = wsum_in[...].astype(jnp.float32) * (1.0 / math.sqrt(8192.0))


def layer(which, share, tiles, feat, weight, bias, cot):
    bf16, f32 = jnp.bfloat16, jnp.float32
    V = pltpu.VMEM
    dma = pltpu.SemaphoreType.DMA
    sizes = [n for _, n in ROWS]
    scratch = [V(tiles.shape, bf16), V((4, 4, 4, 128, 256), bf16)]
    scratch += [V((4, 256, 16 * n), bf16) for n in sizes]
    scratch += [V((256, 256), bf16)]
    scratch += [V((4, 4, 4, 2, n, 128), bf16) for n in sizes]
    scratch += [V((4, 4, 4, 2, n, 128), bf16) for n in sizes]
    scratch += [V((2, 3, 4, 4, n, 128), bf16) for n in sizes]
    scratch += [V((2, 3, 4, n, 128), bf16) for n in sizes]
    scratch += [V((3, 2, n, 128), bf16) for n in sizes]
    scratch += [V((128, 512), bf16)] * 3
    scratch += [V((4, 4, 4, 16, 128), bf16)]
    scratch += [V((3, 4, 4, 16, 128), bf16), V((3, 4, 16, 128), bf16), V((3, 16, 128), bf16)]
    scratch += [V((4, 4, 4, 16, 128), bf16), V((256, 256), f32)]
    scratch += [dma((1,)), dma((4,)), dma((4,)), dma((1,)), dma((1,))]
    scratch += [dma((3, 2, 2, 6))] * 2 + [dma((3, 3))] * 4
    scratch += [dma((3, 2, 4, 2, 3))] * 2 + [dma((3, 3))] * 4
    whole = pl.BlockSpec(memory_space=pltpu.VMEM)
    return pl.pallas_call(
        layer_kernel,
        out_shape=[
            jax.ShapeDtypeStruct((128, 256), bf16),
            jax.ShapeDtypeStruct((512, 256), bf16),
            jax.ShapeDtypeStruct((128, 256), bf16),
        ],
        in_specs=[pl.BlockSpec(memory_space=pltpu.SMEM)] * 2 + [pl.BlockSpec(memory_space=pl.ANY)] + [whole] * 4,
        out_specs=[whole] * 3,
        scratch_shapes=scratch,
        compiler_params=pltpu.CompilerParams(collective_id=0, has_side_effects=True),
        name="layer",
    )(which, share, tiles, feat, weight, bias, cot)


def per_device(features, tiles, tile_dest, tile_count, weight, bias, cotangent):
    domains = lax.axis_size("dom")
    which, share = tile_index(tile_dest[:, 0], tile_count, domains)
    act, wsum, fgrad = layer(which, share, tiles, features, weight, bias.reshape(1, -1), cotangent)
    whole = pl.BlockSpec(memory_space=pltpu.VMEM)
    return pl.pallas_call(
        finish,
        out_shape=[
            jax.ShapeDtypeStruct(act.shape, act.dtype),
            jax.ShapeDtypeStruct(wsum.shape, jnp.float32),
            jax.ShapeDtypeStruct(fgrad.shape, fgrad.dtype),
        ],
        in_specs=[whole] * 3,
        out_specs=[whole] * 3,
        name="finish",
    )(act, wsum, fgrad)


def solution(mesh):
    in_specs = (
        P("dom", None),
        P(("rep", "dom"), None, None),
        P(("rep", "dom"), None),
        P(("rep", "dom")),
        P(),
        P(),
        P("dom", None),
    )
    out_specs = (P("dom", "rep"), P(None, "rep"), P("dom", "rep"))
    return jax.shard_map(
        per_device, mesh=mesh, in_specs=in_specs, out_specs=out_specs, check_vma=False
    )
```
